768 devices in a mesh: seq: 96 (over y, z), head: 8 (over x, core).
Axes of the slice: x: 4, y: 8, z: 12, core: 2. Of those that a mesh axis runs over, the one named last changes fastest.
Arguments:
- queries: bfloat16 [12288, 2048], P('seq', 'head'), may hold values from -6 to 6
- keys: bfloat16 [12288, 2048], P('seq', 'head'), may hold values from -6 to 6
- values: bfloat16 [12288, 2048], P('seq', 'head'), may hold values from -6 to 6
- grad_out: bfloat16 [12288, 2048], P('seq', 'head'), may hold values from -6 to 6
- gain: float32 [2048], P('head'), may hold values from 0.1 to 1.9
- segment_ids: int32 [96, 128], P('seq'), may hold values from 0 to 7, never falling along the last dimension, each value on 1 to 32 neighbouring positions
Outputs:
- output: bfloat16 [12288, 2048], P('seq', 'head')
- grad_queries: bfloat16 [12288, 2048], P('seq', 'head')
- grad_keys: bfloat16 [12288, 2048], P('seq', 'head')
- grad_values: bfloat16 [12288, 2048], P('seq', 'head')
The draws below stay inside these ranges and needn't reach their ends.
Inputs may be any that keep to these rules, and one draw needn't show every extreme that they name: `segment_ids`: ids never fall along a group; each mask block holds 1 to 32 tokens, one exactly 32.
All inputs are finite; a program needn't handle non-finite values.
Results may differ from the reference program's by a relative error of at most 0.0058.
Values sent between devices are 32-bit elements; how exact they have to be, the bound alone decides.
No kernel may reach another device: no remote copies, remote signals or barrier semaphores. Data moves between devices by JAX's collectives and lax.ppermute only.
A program may use at most 32 MiB of HBM per device.

```python
import math
import jax
import jax.numpy as jnp
import numpy as np
from jax import lax

HEADS = 16
HD = 128
D = 2048
TOK_DEV = 128
SEG_COUNT = 8
SEG_MOST = 32
GROUPS = 96
TOKENS = 12288


def steps_of(rng, dims, split, low, largest):
    level = 1.0
    for dim, parts in split:
        steps = jax.random.uniform(jax.random.fold_in(jax.random.fold_in(rng, 6), dim), (parts,), jnp.float32, low / len(split), largest / len(split))
        level = level * jnp.repeat(jnp.exp(steps), dims[dim] // parts).reshape((-1,) + (1,) * (len(dims) - 1 - dim))
    return level


def profile(number_of, total, bound, lean):
    loads = [(1 << 20) // math.isqrt(grade ** lean) + 1 for grade in range(2, number_of + 1)]
    rest, holding = total - bound - (number_of - 1), [1] * (number_of - 1)
    while rest > 0:
        candidates = [i for i in range(number_of - 1) if holding[i] < bound]
        pool, left = sum([loads[i] for i in candidates]), rest
        for i in candidates:
            more = min(bound - holding[i], max(1, left * loads[i] // pool), rest)
            holding[i] = holding[i] + more
            rest = rest - more
    return np.array([bound] + holding)


def uneven_parts(stream_key, count, total, most, lean):
    if count == 2:
        one = jax.random.randint(stream_key, (), max(1, total - most), min(most, total - 1) + 1)
        return jnp.stack([one, total - one])
    sizes = jnp.asarray(profile(count, total, most, lean), jnp.int32)
    twos = (count - 1) // 2
    giver, taker = sizes[1:1 + 2 * twos:2], sizes[2:2 + 2 * twos:2]
    slack = jnp.minimum(giver - 1, most - taker)
    passed = jax.random.randint(jax.random.fold_in(stream_key, 1), (twos,), 0, 1 << 20) % (slack + 1)
    sizes = sizes.at[1:1 + 2 * twos:2].set(giver - passed).at[2:2 + 2 * twos:2].set(taker + passed)
    return sizes[jax.random.permutation(jax.random.fold_in(stream_key, 2), count)]


def bell_draw(rng, extent, spread, most, pieces=(), held_as=jnp.bfloat16):
    values = jax.random.normal(rng, extent, jnp.float32) * spread
    if len(pieces) > 0:
        values = steps_of(rng, extent, pieces, -0.22, 0.18) * values
    return jnp.clip(values, min=-most, max=most).astype(held_as)


def setup_inputs(seed: int = 0) -> dict:
    streams_of = jax.random.split(jax.random.key(seed), 7)
    queries = bell_draw(streams_of[0], (TOKENS, D), 1.0, 6.0, ((0, 96), (1, 8)))
    keys = bell_draw(streams_of[1], (TOKENS, D), 1.0, 6.0, ((0, 96), (1, 8)))
    values = bell_draw(streams_of[2], (TOKENS, D), 1.0, 6.0, ((0, 96), (1, 8)))
    grad_out = bell_draw(streams_of[3], (TOKENS, D), 1.0, 6.0, ((0, 96), (1, 8)))
    gain = jnp.clip(1.0 + 0.18 * jax.random.normal(streams_of[4], (D,), jnp.float32), 0.1, 1.9)
    segment_ids = jax.vmap(lambda own: jnp.searchsorted(jnp.cumsum(uneven_parts(own, SEG_COUNT, TOK_DEV, SEG_MOST, 2)), jnp.arange(TOK_DEV), side="right"))(jax.random.split(streams_of[5], GROUPS)).reshape((GROUPS, TOK_DEV)).astype(jnp.int32)
    return dict(queries=queries, keys=keys, values=values, grad_out=grad_out, gain=gain, segment_ids=segment_ids)


def rounded(x):
    return lax.optimization_barrier(x.astype(jnp.bfloat16)).astype(jnp.float32)

def block_mask(segment):
    row_ids = lax.broadcasted_iota(jnp.int32, (TOK_DEV, TOK_DEV), 0)
    col_ids = lax.broadcasted_iota(jnp.int32, (TOK_DEV, TOK_DEV), 1)
    same = segment[:, None] == segment[None, :]
    return jnp.where(same & (col_ids <= row_ids), 1.0, 0.0).astype(jnp.float32)

def reference(queries, keys, values, grad_out, gain, segment_ids):
    shape4 = (GROUPS, TOK_DEV, HEADS, HD)
    q_all = queries.reshape(shape4)
    k_all = keys.reshape(shape4)
    v_all = values.reshape(shape4)
    dy_all = grad_out.reshape(GROUPS, TOK_DEV, D)
    gain_f = gain.astype(jnp.float32)

    def forward(carry, inputs):
        q_c, k_c, v_c, dy_c, segment = inputs
        allowed = block_mask(segment)
        q_f = q_c.astype(jnp.float32)
        k_f = k_c.astype(jnp.float32)
        v_f = v_c.astype(jnp.float32)
        scores = rounded(jnp.einsum('thd,shd->hts', q_f, k_f) * allowed[None])
        attn = jnp.einsum('hts,she->the', scores, v_f) + jnp.einsum('thd,hde->the', q_f, rounded(carry))
        flat = attn.reshape(TOK_DEV, D)
        inverse = lax.rsqrt(lax.optimization_barrier(jnp.sum(flat * flat, axis=1)) / D + 1e-06)
        out_c = (gain_f * flat * inverse[:, None]).astype(jnp.bfloat16)
        gained = gain_f * dy_c.astype(jnp.float32)
        products = lax.optimization_barrier(jnp.sum(gained * flat, axis=1))
        dflat = gained * inverse[:, None] - flat * (products * inverse ** 3 / D)[:, None]
        dattn = dflat.astype(jnp.bfloat16)
        dattn_f = dattn.astype(jnp.float32).reshape(TOK_DEV, HEADS, HD)
        grad_local = jnp.einsum('thd,the->hde', q_f, dattn_f)
        new_carry = carry + jnp.einsum('thd,the->hde', k_f, v_f)
        return (new_carry, (out_c, dattn, carry, grad_local))
    start = jnp.zeros((HEADS, HD, HD), jnp.float32)
    ignored, (outs, dattns, states, grads) = lax.scan(forward, start, (q_all, k_all, v_all, dy_all, segment_ids))

    def backward_sum(carry, grad_local):
        return (carry + grad_local, carry)
    ignored2, laters = lax.scan(backward_sum, start, grads, reverse=True)

    def backward(inputs):
        q_c, k_c, v_c, dattn, segment, state, later = inputs
        allowed = block_mask(segment)
        q_f = q_c.astype(jnp.float32)
        k_f = k_c.astype(jnp.float32)
        v_f = v_c.astype(jnp.float32)
        dattn_f = dattn.astype(jnp.float32).reshape(TOK_DEV, HEADS, HD)
        scores = rounded(jnp.einsum('thd,shd->hts', q_f, k_f) * allowed[None])
        dscores = rounded(jnp.einsum('the,she->hts', dattn_f, v_f) * allowed[None])
        state_b = rounded(state)
        later_b = rounded(later)
        grad_q = jnp.einsum('hts,shd->thd', dscores, k_f) + jnp.einsum('the,hde->thd', dattn_f, state_b)
        grad_k = jnp.einsum('hts,thd->shd', dscores, q_f) + jnp.einsum('she,hde->shd', v_f, later_b)
        grad_v = jnp.einsum('hts,the->she', scores, dattn_f) + jnp.einsum('shd,hde->she', k_f, later_b)
        return (grad_q.reshape(TOK_DEV, D).astype(jnp.bfloat16), grad_k.reshape(TOK_DEV, D).astype(jnp.bfloat16), grad_v.reshape(TOK_DEV, D).astype(jnp.bfloat16))
    grad_q, grad_k, grad_v = lax.map(backward, (q_all, k_all, v_all, dattns, segment_ids, states, laters))
    return (outs.reshape(TOKENS, D), grad_q.reshape(TOKENS, D), grad_k.reshape(TOKENS, D), grad_v.reshape(TOKENS, D))
```

```python
import jax
import jax.numpy as jnp
from jax import lax
from jax.sharding import PartitionSpec as P

HD = 128
D = 2048
NY, NZ = 8, 12
BY, BZ = 4, 4
AY, AZ = NY // BY, NZ // BZ
MEMBERS = BY * BZ
BLOCKS = AY * AZ
ROWS = 2 * HD // MEMBERS

INSIDE = [
    [(BY * a + i) * NZ + BZ * b + j for i in range(BY) for j in range(BZ)]
    for a in range(AY)
    for b in range(AZ)
]
ACROSS = [
    [(BY * a + i) * NZ + BZ * b + j for a in range(AY) for b in range(AZ)]
    for i in range(BY)
    for j in range(BZ)
]


def carried(local, later):
    position = lax.axis_index("seq")
    a = (position // NZ) // BY
    b = (position % NZ) // BZ
    parts = local.reshape(MEMBERS, ROWS, HD)
    parts = lax.all_to_all(parts, "seq", 0, 0, axis_index_groups=INSIDE)
    parts = parts.reshape(BY, BZ, ROWS, HD)
    row = jnp.sum(parts, axis=1)
    block = jnp.arange(BLOCKS)
    to_a, to_b = block // AZ, block % AZ
    if later:
        whole = to_a < a
        same_row = (to_a == a) & (to_b < b)
    else:
        whole = to_a > a
        same_row = (to_a == a) & (to_b > b)
    same = to_a == a
    own = jnp.arange(BY)
    other = own[None, :] > own[:, None] if later else own[None, :] < own[:, None]
    eye = own[None, :] == own[:, None]
    counted = (
        whole[:, None, None]
        | (same[:, None, None] & other[None])
        | (same_row[:, None, None] & eye[None])
    )
    sent = jnp.sum(jnp.where(counted[:, :, :, None, None], row[None, None], 0.0), axis=2)
    got = lax.all_to_all(sent, "seq", 0, 0, axis_index_groups=ACROSS)
    base = jnp.sum(got, axis=0)
    out = []
    order = range(BZ - 1, -1, -1) if later else range(BZ)
    running = base
    for j in order:
        running = running + parts[:, j]
        out.append(running)
    if later:
        out = out[::-1]
    back = jnp.stack(out, axis=1).reshape(MEMBERS, ROWS, HD)
    back = lax.all_to_all(back, "seq", 0, 0, axis_index_groups=INSIDE)
    return back.reshape(local.shape) - local


def on_device(queries, keys, values, grad_out, gain, segment_ids):
    length = queries.shape[0]
    width = queries.shape[1]
    heads_here = width // HD
    queries_h = queries.reshape(length, heads_here, HD)
    keys_h = keys.reshape(length, heads_here, HD)
    values_h = values.reshape(length, heads_here, HD)
    segment = segment_ids[0]
    row_ids = lax.broadcasted_iota(jnp.int32, (length, length), 0)
    col_ids = lax.broadcasted_iota(jnp.int32, (length, length), 1)
    allowed = jnp.where(
        (segment[:, None] == segment[None, :]) & (col_ids <= row_ids), 1.0, 0.0
    ).astype(jnp.float32)
    raw_scores = jnp.einsum("thd,shd->hts", queries_h, keys_h, preferred_element_type=jnp.float32)
    scores = (raw_scores * allowed[None]).astype(jnp.bfloat16)
    local_state = jnp.einsum("thd,the->hde", keys_h, values_h, preferred_element_type=jnp.float32)
    state = carried(local_state, False)
    state_b = state.astype(jnp.bfloat16)
    attn = jnp.einsum("hts,she->the", scores, values_h, preferred_element_type=jnp.float32)
    attn = attn + jnp.einsum("thd,hde->the", queries_h, state_b, preferred_element_type=jnp.float32)
    flat = attn.reshape(length, width)
    gained = gain * grad_out.astype(jnp.float32)
    own = jnp.stack([jnp.sum(flat * flat, axis=1), jnp.sum(gained * flat, axis=1)])
    own = jnp.broadcast_to(own[None], (8, 2, length))
    squares, products = jnp.sum(lax.all_to_all(own, "head", 0, 0), axis=0)
    inverse = lax.rsqrt(squares / D + 1e-06)
    output = (gain * flat * inverse[:, None]).astype(jnp.bfloat16)
    dflat = gained * inverse[:, None] - flat * (products * inverse**3 / D)[:, None]
    dattn = dflat.astype(jnp.bfloat16).reshape(length, heads_here, HD)
    grad_local = jnp.einsum("thd,the->hde", queries_h, dattn, preferred_element_type=jnp.float32)
    later = carried(grad_local, True)
    later_b = later.astype(jnp.bfloat16)
    dscores = (
        jnp.einsum("the,she->hts", dattn, values_h, preferred_element_type=jnp.float32)
        * allowed[None]
    ).astype(jnp.bfloat16)
    grad_q = jnp.einsum("hts,shd->thd", dscores, keys_h, preferred_element_type=jnp.float32)
    grad_q = grad_q + jnp.einsum("the,hde->thd", dattn, state_b, preferred_element_type=jnp.float32)
    grad_k = jnp.einsum("hts,thd->shd", dscores, queries_h, preferred_element_type=jnp.float32)
    grad_k = grad_k + jnp.einsum(
        "she,hde->shd", values_h, later_b, preferred_element_type=jnp.float32
    )
    grad_v = jnp.einsum("hts,the->she", scores, dattn, preferred_element_type=jnp.float32)
    grad_v = grad_v + jnp.einsum(
        "shd,hde->she", keys_h, later_b, preferred_element_type=jnp.float32
    )
    return (
        output,
        grad_q.reshape(length, width).astype(jnp.bfloat16),
        grad_k.reshape(length, width).astype(jnp.bfloat16),
        grad_v.reshape(length, width).astype(jnp.bfloat16),
    )


def solution(mesh):
    placed = (
        P("seq", "head"),
        P("seq", "head"),
        P("seq", "head"),
        P("seq", "head"),
        P("head"),
        P("seq", None),
    )
    return jax.shard_map(
        on_device,
        mesh=mesh,
        in_specs=placed,
        out_specs=(P("seq", "head"), P("seq", "head"), P("seq", "head"), P("seq", "head")),
        check_vma=False,
    )
```

```python
import functools

import jax
import jax.numpy as jnp
from jax import lax
from jax.experimental import pallas as pl
from jax.experimental.pallas import tpu as pltpu
from jax.sharding import PartitionSpec as P

HD = 128
D = 2048
NY, NZ = 8, 12
BZ = 4
AZ = NZ // BZ
MEMBERS = NY * BZ
ROWS = 2 * HD // MEMBERS

ORDER = [26, 17, 11, 10, 28, 1, 5, 4, 7, 16, 9, 19, 30, 13, 22, 0, 21, 29, 6, 12, 20, 23, 14, 15, 3, 31, 2, 24, 25, 27, 18, 8]
SLOT = [[ORDER.index(BZ * y + z) for z in range(BZ)] for y in range(NY)]
INSIDE = [[(k // BZ) * NZ + BZ * b + k % BZ for k in ORDER] for b in range(AZ)]
ACROSS = [
    [y * NZ + BZ * b + z for b in range(AZ)][:: 1 if z % 2 else -1]
    for y in range(NY)
    for z in range(BZ)
]


def spread_kernel(later, parts_ref, sent_ref):
    column = lax.axis_index("seq") % NZ
    b = column // BZ
    flip = 1 - column % 2
    rows = []
    for y in range(NY):
        row = parts_ref[SLOT[y][0]]
        for z in range(1, BZ):
            row = row + parts_ref[SLOT[y][z]]
        rows.append(row)
    running = jnp.zeros_like(rows[0])
    for y in range(NY - 1, -1, -1) if later else range(NY):
        for to in range(AZ):
            dest = jnp.where(flip == 1, AZ - 1 - to, to)
            takes = dest < b if later else dest > b
            sent_ref[to, y] = running + jnp.where(takes, rows[y], 0.0)
        running = running + rows[y]


def finish_kernel(later, parts_ref, got_ref, back_ref):
    for y in range(NY):
        running = got_ref[0, y]
        for src in range(1, AZ):
            running = running + got_ref[src, y]
        for z in range(BZ - 1, -1, -1) if later else range(BZ):
            running = running + parts_ref[SLOT[y][z]]
            back_ref[SLOT[y][z]] = running


def in_vmem(x):
    return pltpu.with_memory_space_constraint(x, pltpu.VMEM)


def carried(local, later):
    vmem = pl.BlockSpec(memory_space=pltpu.VMEM)
    parts = local.reshape(MEMBERS, ROWS, HD)
    parts = lax.all_to_all(parts, "seq", 0, 0, axis_index_groups=INSIDE)
    sent = pl.pallas_call(
        functools.partial(spread_kernel, later),
        out_shape=pltpu.VMEM((AZ, NY, ROWS, HD), jnp.float32),
        in_specs=[vmem],
        out_specs=vmem,
        name="spread_later" if later else "spread",
    )(in_vmem(parts))
    got = lax.all_to_all(sent, "seq", 0, 0, axis_index_groups=ACROSS)
    back = pl.pallas_call(
        functools.partial(finish_kernel, later),
        out_shape=pltpu.VMEM((MEMBERS, ROWS, HD), jnp.float32),
        in_specs=[vmem, vmem],
        out_specs=vmem,
        name="finish_later" if later else "finish",
    )(in_vmem(parts), in_vmem(got))
    back = lax.all_to_all(back, "seq", 0, 0, axis_index_groups=INSIDE)
    return back.reshape(local.shape) - local


def on_device(queries, keys, values, grad_out, gain, segment_ids):
    length = queries.shape[0]
    width = queries.shape[1]
    heads_here = width // HD
    queries_h = queries.reshape(length, heads_here, HD)
    keys_h = keys.reshape(length, heads_here, HD)
    values_h = values.reshape(length, heads_here, HD)
    segment = segment_ids[0]
    row_ids = lax.broadcasted_iota(jnp.int32, (length, length), 0)
    col_ids = lax.broadcasted_iota(jnp.int32, (length, length), 1)
    allowed = jnp.where(
        (segment[:, None] == segment[None, :]) & (col_ids <= row_ids), 1.0, 0.0
    ).astype(jnp.float32)
    raw_scores = jnp.einsum("thd,shd->hts", queries_h, keys_h, preferred_element_type=jnp.float32)
    scores = (raw_scores * allowed[None]).astype(jnp.bfloat16)
    local_state = jnp.einsum("thd,the->hde", keys_h, values_h, preferred_element_type=jnp.float32)
    state = carried(local_state, False)
    state_b = state.astype(jnp.bfloat16)
    attn = jnp.einsum("hts,she->the", scores, values_h, preferred_element_type=jnp.float32)
    attn = attn + jnp.einsum("thd,hde->the", queries_h, state_b, preferred_element_type=jnp.float32)
    flat = attn.reshape(length, width)
    gained = gain * grad_out.astype(jnp.float32)
    own = jnp.stack([jnp.sum(flat * flat, axis=1), jnp.sum(gained * flat, axis=1)])
    own = jnp.broadcast_to(own[None], (8, 2, length))
    squares, products = jnp.sum(lax.all_to_all(own, "head", 0, 0), axis=0)
    inverse = lax.rsqrt(squares / D + 1e-06)
    output = (gain * flat * inverse[:, None]).astype(jnp.bfloat16)
    dflat = gained * inverse[:, None] - flat * (products * inverse**3 / D)[:, None]
    dattn = dflat.astype(jnp.bfloat16).reshape(length, heads_here, HD)
    grad_local = jnp.einsum("thd,the->hde", queries_h, dattn, preferred_element_type=jnp.float32)
    later = carried(grad_local, True)
    later_b = later.astype(jnp.bfloat16)
    dscores = (
        jnp.einsum("the,she->hts", dattn, values_h, preferred_element_type=jnp.float32)
        * allowed[None]
    ).astype(jnp.bfloat16)
    grad_q = jnp.einsum("hts,shd->thd", dscores, keys_h, preferred_element_type=jnp.float32)
    grad_q = grad_q + jnp.einsum("the,hde->thd", dattn, state_b, preferred_element_type=jnp.float32)
    grad_k = jnp.einsum("hts,thd->shd", dscores, queries_h, preferred_element_type=jnp.float32)
    grad_k = grad_k + jnp.einsum(
        "she,hde->shd", values_h, later_b, preferred_element_type=jnp.float32
    )
    grad_v = jnp.einsum("hts,the->she", scores, dattn, preferred_element_type=jnp.float32)
    grad_v = grad_v + jnp.einsum(
        "shd,hde->she", keys_h, later_b, preferred_element_type=jnp.float32
    )
    return (
        output,
        grad_q.reshape(length, width).astype(jnp.bfloat16),
        grad_k.reshape(length, width).astype(jnp.bfloat16),
        grad_v.reshape(length, width).astype(jnp.bfloat16),
    )


def solution(mesh):
    placed = (
        P("seq", "head"),
        P("seq", "head"),
        P("seq", "head"),
        P("seq", "head"),
        P("head"),
        P("seq", None),
    )
    return jax.shard_map(
        on_device,
        mesh=mesh,
        in_specs=placed,
        out_specs=(P("seq", "head"), P("seq", "head"), P("seq", "head"), P("seq", "head")),
        check_vma=False,
    )
```

```python
import functools

import jax
import jax.numpy as jnp
from jax import lax
from jax.experimental import pallas as pl
from jax.experimental.pallas import tpu as pltpu
from jax.sharding import PartitionSpec as P

HD = 128
D = 2048
TOK = 128
NY, NZ = 8, 12
BZ = 4
AZ = NZ // BZ
MEMBERS = NY * BZ
ROWS = 2 * HD // MEMBERS

ORDER = [22, 17, 11, 10, 28, 1, 5, 4, 7, 16, 9, 19, 30, 13, 26, 0, 21, 29, 6, 12, 20, 23, 14, 15, 3, 31, 2, 24, 25, 27, 18, 8]
SLOT = [[ORDER.index(BZ * y + z) for z in range(BZ)] for y in range(NY)]
INSIDE = [[(k // BZ) * NZ + BZ * b + k % BZ for k in ORDER] for b in range(AZ)]
ACROSS = [
    [y * NZ + BZ * b + z for b in range(AZ)][:: 1 if z % 2 else -1]
    for y in range(NY)
    for z in range(BZ)
]


def spread_kernel(later, parts_ref, sent_ref):
    column = lax.axis_index("seq") % NZ
    b = column // BZ
    flip = 1 - column % 2
    rows = []
    for y in range(NY):
        row = parts_ref[SLOT[y][0]]
        for z in range(1, BZ):
            row = row + parts_ref[SLOT[y][z]]
        rows.append(row)
    running = jnp.zeros_like(rows[0])
    for y in range(NY - 1, -1, -1) if later else range(NY):
        for to in range(AZ):
            dest = jnp.where(flip == 1, AZ - 1 - to, to)
            takes = dest < b if later else dest > b
            sent_ref[to, y] = running + jnp.where(takes, rows[y], 0.0)
        running = running + rows[y]


def finish_kernel(later, parts_ref, got_ref, back_ref):
    for y in range(NY):
        running = got_ref[0, y]
        for src in range(1, AZ):
            running = running + got_ref[src, y]
        for z in range(BZ - 1, -1, -1) if later else range(BZ):
            back_ref[SLOT[y][z]] = running
            running = running + parts_ref[SLOT[y][z]]


def dot(a, b, contract):
    return lax.dot_general(a, b, (contract, ((), ())), preferred_element_type=jnp.float32)


def state_kernel(keys_ref, values_ref, out_ref):
    for h in range(2):
        cols = slice(HD * h, HD * h + HD)
        local = dot(keys_ref[:, cols], values_ref[:, cols], ((0,), (0,)))
        out_ref[16 * h : 16 * h + 16] = local.reshape(16, ROWS, HD)


def inner_kernel(
    segment_ref, gain_in_ref, queries_ref, keys_ref, values_ref, scores_ref, intra_ref, gain_ref
):
    gain_ref[...] = jnp.broadcast_to(gain_in_ref[...], gain_ref.shape)
    allowed = mask_of(segment_ref)
    for h in range(2):
        cols = slice(HD * h, HD * h + HD)
        raw = dot(queries_ref[:, cols], keys_ref[:, cols], ((1,), (1,)))
        scores = (raw * allowed).astype(jnp.bfloat16)
        scores_ref[h] = scores
        intra_ref[:, cols] = dot(scores, values_ref[:, cols], ((1,), (0,)))


def mask_of(segment_ref):
    across = jnp.broadcast_to(segment_ref[...], (TOK, TOK))
    row_ids = lax.broadcasted_iota(jnp.int32, (TOK, TOK), 0)
    col_ids = lax.broadcasted_iota(jnp.int32, (TOK, TOK), 1)
    return jnp.where((across.T == across) & (col_ids <= row_ids), 1.0, 0.0)


def state_of(state_ref, h):
    return state_ref[16 * h : 16 * h + 16].reshape(HD, HD).astype(jnp.bfloat16)


def attention(intra_ref, queries_ref, state_ref, h):
    cols = slice(HD * h, HD * h + HD)
    return intra_ref[:, cols] + dot(queries_ref[:, cols], state_of(state_ref, h), ((1,), (0,)))


def attend_kernel(intra_ref, queries_ref, state_ref, grad_ref, gain_ref, own_ref):
    squares = jnp.zeros((TOK, 1), jnp.float32)
    products = jnp.zeros((TOK, 1), jnp.float32)
    for h in range(2):
        cols = slice(HD * h, HD * h + HD)
        flat = attention(intra_ref, queries_ref, state_ref, h)
        gained = gain_ref[0:1, cols] * grad_ref[:, cols].astype(jnp.float32)
        squares = squares + jnp.sum(flat * flat, axis=1, keepdims=True)
        products = products + jnp.sum(gained * flat, axis=1, keepdims=True)
    lane = lax.broadcasted_iota(jnp.int32, (TOK, HD), 1)
    turned = jnp.where(lane == 0, squares, products).T[:8]
    for k in range(8):
        own_ref[k] = turned


def norm_of(got_ref):
    total = got_ref[0]
    for k in range(1, 8):
        total = total + got_ref[k]
    inverse = lax.rsqrt(total[0:1] / D + 1e-06)
    scaled = total[1:2] * inverse**3 / D
    row = lax.broadcasted_iota(jnp.int32, (HD, TOK), 0)
    turned = jnp.where(row == 0, inverse, scaled).T
    return turned[:, 0:1], turned[:, 1:2]


def gradient_kernel(
    got_ref, intra_ref, queries_ref, state_ref, grad_ref, gain_ref, out_ref, dattn_ref
):
    inverse, scaled = norm_of(got_ref)
    for h in range(2):
        cols = slice(HD * h, HD * h + HD)
        flat = attention(intra_ref, queries_ref, state_ref, h)
        gained = gain_ref[0:1, cols] * grad_ref[:, cols].astype(jnp.float32)
        dattn = (gained * inverse - flat * scaled).astype(jnp.bfloat16)
        dattn_ref[:, cols] = dattn
        local = dot(queries_ref[:, cols], dattn, ((0,), (0,)))
        out_ref[16 * h : 16 * h + 16] = local.reshape(16, ROWS, HD)


def local_kernel(
    segment_ref,
    queries_ref,
    keys_ref,
    values_ref,
    scores_ref,
    state_ref,
    dattn_ref,
    got_ref,
    intra_ref,
    gain_ref,
    output_ref,
    grad_q_ref,
    part_k_ref,
    part_v_ref,
):
    allowed = mask_of(segment_ref)
    inverse = norm_of(got_ref)[0]
    for h in range(2):
        cols = slice(HD * h, HD * h + HD)
        flat = attention(intra_ref, queries_ref, state_ref, h)
        output_ref[:, cols] = (gain_ref[0:1, cols] * flat * inverse).astype(jnp.bfloat16)
        dattn = dattn_ref[:, cols]
        raw = dot(dattn, values_ref[:, cols], ((1,), (1,)))
        dscores = (raw * allowed).astype(jnp.bfloat16)
        grad_q = dot(dscores, keys_ref[:, cols], ((1,), (0,)))
        grad_q = grad_q + dot(dattn, state_of(state_ref, h), ((1,), (1,)))
        grad_q_ref[:, cols] = grad_q.astype(jnp.bfloat16)
        part_k_ref[:, cols] = dot(dscores, queries_ref[:, cols], ((0,), (0,)))
        part_v_ref[:, cols] = dot(scores_ref[h], dattn, ((0,), (0,)))


def closing_kernel(
    later_ref, keys_ref, values_ref, part_k_ref, part_v_ref, grad_k_ref, grad_v_ref
):
    for h in range(2):
        cols = slice(HD * h, HD * h + HD)
        later_b = later_ref[16 * h : 16 * h + 16].reshape(HD, HD).astype(jnp.bfloat16)
        grad_k = part_k_ref[:, cols] + dot(values_ref[:, cols], later_b, ((1,), (1,)))
        grad_k_ref[:, cols] = grad_k.astype(jnp.bfloat16)
        grad_v = part_v_ref[:, cols] + dot(keys_ref[:, cols], later_b, ((1,), (0,)))
        grad_v_ref[:, cols] = grad_v.astype(jnp.bfloat16)


def on_chip(body, outs, *args, leaving=0):
    vmem = pl.BlockSpec(memory_space=pltpu.VMEM)
    return pl.pallas_call(
        body,
        out_shape=tuple(
            jax.ShapeDtypeStruct(shape, dtype) if k < leaving else pltpu.VMEM(shape, dtype)
            for k, (shape, dtype) in enumerate(outs)
        ),
        in_specs=[vmem] * len(args),
        out_specs=(vmem,) * len(outs),
    )(*[pltpu.with_memory_space_constraint(x, pltpu.VMEM) for x in args])


PARTS = ((MEMBERS, ROWS, HD), jnp.float32)


def carried(parts, later):
    parts = lax.all_to_all(parts, "seq", 0, 0, axis_index_groups=INSIDE)
    (sent,) = on_chip(
        functools.partial(spread_kernel, later), [((AZ, NY, ROWS, HD), jnp.float32)], parts
    )
    got = lax.all_to_all(sent, "seq", 0, 0, axis_index_groups=ACROSS)
    (back,) = on_chip(functools.partial(finish_kernel, later), [PARTS], parts, got)
    return lax.all_to_all(back, "seq", 0, 0, axis_index_groups=INSIDE)


def on_device(queries, keys, values, grad_out, gain, segment_ids):
    length, width = queries.shape
    wide = (length, width)
    heads = (width // HD, length, length)
    vmem = pl.BlockSpec(memory_space=pltpu.VMEM)
    local_state = pl.pallas_call(
        state_kernel,
        out_shape=jax.ShapeDtypeStruct(*PARTS),
        in_specs=[vmem, vmem],
        out_specs=vmem,
        name="state",
    )(keys, values)
    scores, intra, gains = on_chip(
        inner_kernel,
        [(heads, jnp.bfloat16), (wide, jnp.float32), ((8, width), jnp.float32)],
        segment_ids,
        gain.reshape(1, width),
        queries,
        keys,
        values,
    )
    state = carried(local_state, False)
    own = on_chip(
        attend_kernel, [((8, 8, HD), jnp.float32)], intra, queries, state, grad_out, gains
    )[0]
    got = lax.all_to_all(own, "head", 0, 0)
    grad_local, dattn = on_chip(
        gradient_kernel, [PARTS, (wide, jnp.bfloat16)], got, intra, queries, state, grad_out, gains
    )
    later = carried(grad_local, True)
    output, grad_q, part_k, part_v = on_chip(
        local_kernel,
        [(wide, jnp.bfloat16)] * 2 + [(wide, jnp.float32)] * 2,
        segment_ids,
        queries,
        keys,
        values,
        scores,
        state,
        dattn,
        got,
        intra,
        gains,
        leaving=2,
    )
    grad_k, grad_v = on_chip(
        closing_kernel,
        [(wide, jnp.bfloat16), (wide, jnp.bfloat16)],
        later,
        keys,
        values,
        part_k,
        part_v,
        leaving=2,
    )
    return output, grad_q, grad_k, grad_v


def solution(mesh):
    placed = (
        P("seq", "head"),
        P("seq", "head"),
        P("seq", "head"),
        P("seq", "head"),
        P("head"),
        P("seq", None),
    )
    return jax.shard_map(
        on_device,
        mesh=mesh,
        in_specs=placed,
        out_specs=(P("seq", "head"), P("seq", "head"), P("seq", "head"), P("seq", "head")),
        check_vma=False,
    )
```
